32 devices in a mesh: groups: 2 (over x), expert: 16 (over z, y, core).
Axes of the slice: x: 2, y: 2, z: 4, core: 2. Of those that a mesh axis runs over, the one named last changes fastest.
Arguments:
- tokens: bfloat16 [4096, 4096], P(('groups', 'expert')), parts along dimension 0, may hold values from -6 to 6
- expert_ids: int32 [4096, 8], P(('groups', 'expert')), parts along dimension 0, may hold values from 0 to 127, all different within a row; in each aligned block of 128 rows (0 to 127, 128 to 255, ...) at most 16 rows name the same one
- levels: int32 [4096, 8], P(('groups', 'expert')), parts along dimension 0, may hold values from 1 to 255
- gate_w: bfloat16 [16, 4096, 384], P('expert'), may hold values from -0.09375 to 0.09375
- up_w: bfloat16 [16, 4096, 384], P('expert'), may hold values from -0.09375 to 0.09375
- down_w: bfloat16 [16, 384, 4096], P('expert'), may hold values from -1.25 to 1.25
Outputs:
- scored: bfloat16 [4096, 4096], P(('groups', 'expert')), parts along dimension 0
The draws below stay inside these ranges and needn't reach their ends.
There are 2 independent parts, one for each index of `groups`. The reference program is written for one: setup_inputs(seed, part) draws one part's arguments, and reference() takes and returns one part's arrays. A program takes and returns all parts, laid end to end along the dimension named above; an argument that names none is the same for every part. Nothing has to cross between parts.
Inputs may be any that keep to these rules, and one draw needn't show every extreme that they name: `expert_ids`: each row names 8 different experts; within the rows of one device no expert is named by more than 16 rows.
All inputs are finite; a program needn't handle non-finite values.
Results may differ from the reference program's by a relative error of at most 0.0075.
Values may be sent and summed in bfloat16 or wider, within the bound.
No kernel may reach another device: no remote copies, remote signals or barrier semaphores. Data moves between devices by JAX's collectives and lax.ppermute only.
A program may use at most 128 MiB of HBM per device.

```python
import math
import jax
import jax.numpy as jnp
import numpy as np
from jax import lax

D = 4096
FF = 1536
EXPERTS = 128
TOPK = 8
SLICES = 4
TOK_DEV = 128
CAP = 16
HS = 384
EXP_WIN = 4
TOKENS = 2048
N_EXPERT = 16


def touch_ends(entries, own_key, low, high):
    place = [jax.random.randint(jax.random.fold_in(own_key, axis), (), 0, length) for axis, length in enumerate(entries.shape)]
    longest = entries.shape.index(max(entries.shape))
    beside = place[:longest] + [(place[longest] + 1) % entries.shape[longest]] + place[longest + 1:]
    return entries.at[tuple(place)].set(low).at[tuple(beside)].set(high)


def level_of(own_key, shape, split, smallest, top_value):
    level, own = 1.0, jax.random.fold_in(own_key, 6)
    for dim, shards_of in split:
        draws = jnp.exp(jax.random.uniform(jax.random.fold_in(own, dim), (shards_of,), jnp.float32, smallest / len(split), top_value / len(split)))
        level = level * jnp.repeat(draws, shape[dim] // shards_of).reshape([-1 if axis == dim else 1 for axis in range(len(shape))])
    return level


def shared_out(rng, own, number, rows, amount, top, bound, lean):
    order = jax.random.permutation(rng, amount)
    crowded, usual = load_shares(amount, rows * top, bound, lean, True), load_shares(amount, rows * top, bound, lean, False)
    places = jnp.arange(amount)

    def named(sizes, offset_by):
        used = int((sizes > 0).sum())
        fixed = max(1, used // 4)
        moved = fixed + (places - fixed + offset_by * (used - fixed)) % max(1, amount - fixed)
        return jnp.zeros((amount,), jnp.int32).at[order[jnp.where(places < fixed, places, moved)]].set(jnp.asarray(sizes, jnp.int32))

    sizes = jnp.where(number % 4 == 0, named(crowded, number // 4), named(usual, number - number // 4 - 1))
    mixed = jax.random.permutation(jax.random.fold_in(own, 3), amount)
    source_of, receiver = mixed[0:amount // 2 * 2:2], mixed[1:amount // 2 * 2:2]
    slack = jnp.minimum(sizes[source_of] - 1, bound - sizes[receiver]) // 2
    slack = jnp.where((source_of == order[0]) | (receiver == order[0]) | (sizes[receiver] == 0), 0, jnp.maximum(slack, 0))
    moved = jax.random.randint(jax.random.fold_in(own, 4), (amount // 2,), 0, 1 << 20) % (slack + 1)
    sizes = sizes.at[source_of].add(-moved).at[receiver].add(moved)
    labels = jnp.searchsorted(jnp.cumsum(sizes), jnp.arange(rows * top), side="right").astype(jnp.int32)
    grid = labels.reshape(top, rows).T
    grid = grid[jax.random.permutation(jax.random.fold_in(own, 1), rows)]
    offset_by = jax.random.randint(jax.random.fold_in(own, 2), (rows, 1), 0, top)
    return jnp.take_along_axis(grid, (jnp.arange(top)[None, :] + offset_by) % top, axis=1)


def load_shares(count, total, reach, lean, full):
    weights = [(1 << 20) // math.isqrt(grade ** lean) + 1 for grade in range(1, count + 1)]
    largest = reach if full else min(reach, max(-(-total // count), total * weights[0] // sum(weights)))
    least = 1 if total - largest >= count - 1 else 0
    counts, surplus = [largest] + [least] * (count - 1), total - largest - least * (count - 1)
    while surplus > 0:
        candidates = [i for i in range(1, count) if counts[i] < largest] or [i for i in range(1, count) if counts[i] < reach]
        mass, remaining = sum([weights[i] for i in candidates]), surplus
        for i in candidates:
            extra = min(reach - counts[i], max(1, remaining * weights[i] // mass), surplus)
            counts[i] = counts[i] + extra
            surplus = surplus - extra
    return np.array(counts)


def normal_values(own_key, dims, spread, most, shards=(), held_as=jnp.bfloat16):
    result = jax.random.normal(own_key, dims, jnp.float32) * spread
    if len(shards) > 0:
        result = level_of(own_key, dims, shards, -0.22, 0.18) * result
    return jnp.clip(result, min=-most, max=most).astype(held_as)


def setup_inputs(seed: int = 0, part: int = 0) -> dict:
    streams_of = jax.random.split(jax.random.key(seed), 7)
    part_keys = jax.random.split(jax.random.fold_in(streams_of[6], part), 7)
    tokens = normal_values(part_keys[0], (TOKENS, D), 1.0, 6.0, ((0, 16),))
    expert_ids_keys = jax.random.split(jax.random.fold_in(part_keys[1], 1), TOKENS // TOK_DEV)
    expert_ids_turns = jax.random.permutation(jax.random.fold_in(part_keys[1], 3), TOKENS // TOK_DEV)
    expert_ids = jax.vmap(lambda own, number: shared_out(jax.random.fold_in(part_keys[1], 2), own, number, TOK_DEV, EXPERTS, TOPK, CAP, 2))(expert_ids_keys, expert_ids_turns).reshape((TOKENS, TOPK))
    levels = touch_ends(jax.random.randint(part_keys[2], (TOKENS, TOPK), 1, 256), jax.random.fold_in(part_keys[2], 1), 1, 255).astype(jnp.int32)
    gate_w = normal_values(streams_of[3], (N_EXPERT, D, HS), D ** -0.5, 0.09375, ((0, 16),))
    up_w = normal_values(streams_of[4], (N_EXPERT, D, HS), D ** -0.5, 0.09375, ((0, 16),))
    down_w = normal_values(streams_of[5], (N_EXPERT, HS, D), (max(FF // 64, 1)) ** -0.5, 1.25, ((0, 16),))
    return dict(tokens=tokens, expert_ids=expert_ids, levels=levels, gate_w=gate_w, up_w=up_w, down_w=down_w)


def expert_output(packed_rows, gate_w, up_w, down_w, expert_num):
    first = expert_num * SLICES
    gate_blocks = lax.dynamic_slice_in_dim(gate_w, first, SLICES, 0)
    up_blocks = lax.dynamic_slice_in_dim(up_w, first, SLICES, 0)
    down_blocks = lax.dynamic_slice_in_dim(down_w, first, SLICES, 0)
    summed = jnp.zeros((packed_rows.shape[0], packed_rows.shape[1]), jnp.float32)
    for slice_num in range(SLICES):
        gate_act = jnp.dot(packed_rows, gate_blocks[slice_num], preferred_element_type=jnp.float32)
        up_act = jnp.dot(packed_rows, up_blocks[slice_num], preferred_element_type=jnp.float32)
        hidden = (jax.nn.silu(gate_act) * up_act).astype(jnp.bfloat16)
        partial_value = jnp.dot(hidden, down_blocks[slice_num], preferred_element_type=jnp.float32).astype(jnp.bfloat16)
        summed = summed + partial_value.astype(jnp.float32)
    return summed.astype(jnp.bfloat16)


def reference(tokens, expert_ids, levels, gate_w, up_w, down_w):
    token_count = tokens.shape[0]
    level_vals = levels.astype(jnp.float32)
    shares = level_vals / jnp.sum(level_vals, axis=1, keepdims=True)
    owner_block = jnp.arange(token_count, dtype=jnp.int32) // TOK_DEV
    slot_total = N_EXPERT * CAP

    def one_expert(running, expert_num):
        matches = expert_ids == expert_num
        routed = jnp.any(matches, axis=1).astype(jnp.int32)
        gate_of = jnp.sum(jnp.where(matches, shares, jnp.float32(0.0)), axis=1)
        per_block = routed.reshape(N_EXPERT, TOK_DEV)
        slot_rank = (jnp.cumsum(per_block, axis=1) - per_block).reshape(-1).astype(jnp.int32)
        position = jnp.where(routed == 1, owner_block * CAP + slot_rank, slot_total).astype(jnp.int32)
        packed_rows = jnp.zeros((slot_total, tokens.shape[1]), tokens.dtype).at[position].set(tokens, mode="drop")
        merged = expert_output(packed_rows, gate_w, up_w, down_w, expert_num)
        picked = merged[jnp.minimum(position, slot_total - 1)].astype(jnp.float32)
        running = running + jnp.where(routed[:, None] == 1, gate_of[:, None] * picked, jnp.float32(0.0))
        return running, None

    start = jnp.zeros((token_count, tokens.shape[1]), jnp.float32)
    summed_out, _ = lax.scan(one_expert, start, jnp.arange(EXP_WIN, dtype=jnp.int32))
    return summed_out.astype(jnp.bfloat16)
```

```python
import jax
import jax.numpy as jnp
from jax import lax
from jax.sharding import PartitionSpec as P

SLICES = 4
CHUNKS = None


def shards(tokens, expert_ids, levels, gate_w, up_w, down_w):
    device_total = lax.axis_size("expert")
    window = device_total // SLICES
    token_count, width = tokens.shape
    capacity = token_count // 8
    plane = lax.axis_index("expert") // SLICES

    def shift(value, k):
        pairs = [(d, (d + k * SLICES) % device_total) for d in range(device_total)]
        return lax.ppermute(value, "expert", pairs)

    def swap(value, bit):
        return lax.ppermute(value, "expert", [(d, d ^ bit) for d in range(device_total)])

    level_vals = levels.astype(jnp.float32)
    shares = level_vals / jnp.sum(level_vals, axis=1, keepdims=True)
    experts = (plane + jnp.arange(window, dtype=jnp.int32)) % window
    one_hot = expert_ids[:, :, None] == experts[None, None, :]
    routed = jnp.sum(one_hot.astype(jnp.int32), axis=1)
    gate_of = jnp.sum(jnp.where(one_hot, shares[:, :, None], jnp.float32(0.0)), axis=1)
    slot_rank = jnp.cumsum(routed, axis=0) - routed
    slot_hit = (slot_rank.T[:, None, :] == jnp.arange(capacity, dtype=jnp.int32)[None, :, None]) & (
        routed.T[:, None, :] == 1
    )
    hit_bf = slot_hit.astype(jnp.bfloat16)
    packed = jnp.einsum("ect,td->ecd", hit_bf, tokens, preferred_element_type=jnp.float32).astype(jnp.bfloat16)

    def ffn(rows):
        gate_act = jnp.dot(rows, gate_w[0], preferred_element_type=jnp.float32)
        up_act = jnp.dot(rows, up_w[0], preferred_element_type=jnp.float32)
        hidden = (jax.nn.silu(gate_act) * up_act).astype(jnp.bfloat16)
        return jnp.dot(hidden, down_w[0], preferred_element_type=jnp.float32)

    chunks = CHUNKS or [list(range(window))]
    landed = [packed[0]] + [shift(packed[k], k) for k in range(1, window)]
    back = [None] * window
    for chunk in chunks:
        own = jnp.concatenate([landed[k] for k in chunk], 0)
        n = own.shape[0]
        both = jnp.concatenate([own, swap(own, 2)], 0)
        rows = jnp.concatenate([both, swap(both, 1)], 0)
        part = ffn(rows)
        mine = part[: 2 * n] + swap(part[2 * n :].astype(jnp.bfloat16), 1).astype(jnp.float32)
        merged = mine[:n] + swap(mine[n:].astype(jnp.bfloat16), 2).astype(jnp.float32)
        merged = merged.astype(jnp.bfloat16)
        for i, k in enumerate(chunk):
            piece = merged[i * capacity : (i + 1) * capacity]
            back[k] = piece if k == 0 else shift(piece, -k)
    expert_out = jnp.stack(back)
    slot_gate = jnp.sum(slot_hit.astype(jnp.float32) * gate_of.T[:, None, :], axis=2)
    scaled = slot_gate[:, :, None] * expert_out.astype(jnp.float32)
    high_part = lax.optimization_barrier(scaled.astype(jnp.bfloat16))
    low_part = (scaled - high_part.astype(jnp.float32)).astype(jnp.bfloat16)
    scored = jnp.einsum("ect,ecd->td", hit_bf, high_part, preferred_element_type=jnp.float32)
    scored = scored + jnp.einsum("ect,ecd->td", hit_bf, low_part, preferred_element_type=jnp.float32)
    return scored.astype(jnp.bfloat16)


def solution(mesh):
    rows = P(("groups", "expert"), None)
    blocks = P("expert", None, None)
    return jax.shard_map(
        shards, mesh=mesh, in_specs=(rows, rows, rows, blocks, blocks, blocks), out_specs=rows, check_vma=False
    )
```

```python
import jax
import jax.numpy as jnp
from jax import lax
from jax.experimental import pallas as pl
from jax.experimental.pallas import tpu as pltpu
from jax.sharding import PartitionSpec as P

SLICES = 4
CORE, CHIP = 1, 2
VMEM = pl.BlockSpec(memory_space=pltpu.VMEM)
SMEM = pl.BlockSpec(memory_space=pltpu.SMEM)
BF16, F32 = jnp.bfloat16, jnp.float32


def hits_of(plane_ref, ids_ref, window, capacity):
    count = ids_ref.shape[1]
    ids = ids_ref[...]
    plane = plane_ref[0]
    chosen = [jnp.where(ids == (plane ^ k), 1.0, 0.0).astype(F32) for k in range(window)]
    routed = jnp.concatenate([jnp.sum(c, axis=0, keepdims=True) for c in chosen], 0)
    before = lax.broadcasted_iota(jnp.int32, (count, count), 0) < lax.broadcasted_iota(
        jnp.int32, (count, count), 1
    )
    rank = jnp.dot(routed.astype(BF16), before.astype(BF16), preferred_element_type=F32)
    slot = lax.broadcasted_iota(jnp.int32, (capacity, count), 0).astype(F32)
    hits = []
    for k in range(window):
        same = jnp.broadcast_to(rank[k : k + 1], slot.shape) == slot
        there = jnp.broadcast_to(routed[k : k + 1], slot.shape) == 1.0
        hits.append(same & there)
    return chosen, hits


def pack_kernel(window, capacity, plane_ref, ids_ref, tokens_ref, *out_refs):
    _, hits = hits_of(plane_ref, ids_ref, window, capacity)
    for k in range(window):
        hit = jnp.where(hits[k], 1.0, 0.0).astype(BF16)
        out_refs[k][...] = jnp.dot(hit, tokens_ref[...], preferred_element_type=F32).astype(BF16)


def gates_kernel(window, capacity, plane_ref, ids_ref, levels_ref, *out_refs):
    chosen, hits = hits_of(plane_ref, ids_ref, window, capacity)
    levels = levels_ref[...].astype(F32)
    shares = levels / jnp.sum(levels, axis=0, keepdims=True)
    for k in range(window):
        gate = jnp.sum(chosen[k] * shares, axis=0, keepdims=True)
        rest = jnp.where(hits[k], jnp.broadcast_to(gate, hits[k].shape), 0.0)
        for part in range(3):
            piece = rest.astype(BF16)
            out_refs[0][part, k] = piece
            rest = rest - piece.astype(F32)


def ffn_kernel(n, *refs):
    gate_ref, up_ref, down_ref, keep_ref, send_ref = refs[n:]
    rows = jnp.concatenate([r[...] for r in refs[:n]], 0)
    half = rows.shape[0] // 2
    gate_act = jnp.dot(rows, gate_ref[0], preferred_element_type=F32)
    up_act = jnp.dot(rows, up_ref[0], preferred_element_type=F32)
    hidden = (gate_act / (1.0 + jnp.exp(-gate_act)) * up_act).astype(BF16)
    part = jnp.dot(hidden, down_ref[0], preferred_element_type=F32)
    keep_ref[...] = part[:half]
    send_ref[...] = part[half:].astype(BF16)


def combine_kernel(owners, mix_ref, *refs):
    pieces, out_ref = refs[:-1], refs[-1]
    values = jnp.concatenate([r[...] for r in pieces], 0)
    total = jnp.zeros(out_ref.shape, F32)
    for part in range(3):
        mix = jnp.concatenate([mix_ref[part, k] for k in owners], 0)
        total += lax.dot_general(mix, values, (((0,), (0,)), ((), ())), preferred_element_type=F32)
    out_ref[...] = total.astype(BF16)


def shards(tokens, expert_ids, levels, gate_w, up_w, down_w):
    device_total = lax.axis_size("expert")
    window = device_total // SLICES
    token_count, width = tokens.shape
    hidden_width = gate_w.shape[2]
    capacity = token_count // 8
    plane = (lax.axis_index("expert") // SLICES).astype(jnp.int32).reshape(1)
    ids_t, levels_t = expert_ids.T, levels.T

    def send(value, bits):
        return lax.ppermute(value, "expert", [(d, d ^ bits) for d in range(device_total)])

    def shape(rows, dtype=BF16):
        return jax.ShapeDtypeStruct((rows, width), dtype)

    def call(kernel, name, out_shape, args, specs=None, flops=0, nbytes=1 << 20, limit=24 << 20):
        return pl.pallas_call(
            kernel,
            out_shape=out_shape,
            in_specs=specs or [VMEM] * len(args),
            out_specs=jax.tree.map(lambda _: VMEM, out_shape),
            name=name,
            cost_estimate=pl.CostEstimate(flops=flops, bytes_accessed=nbytes, transcendentals=0),
            compiler_params=pltpu.CompilerParams(vmem_limit_bytes=limit),
        )(*args)

    packed = call(
        lambda *r: pack_kernel(window, capacity, *r), "pack",
        [shape(capacity)] * window, (plane, ids_t, tokens), [SMEM, VMEM, VMEM],
        2 * window * capacity * token_count * width,
    )
    far = list(range(2, window))
    half = len(far) // 2
    groups = [g for g in (far[half:], far[:half]) if g]
    landed = {k: send(packed[k], k * SLICES) for g in groups for k in g}
    near = [packed[0], send(packed[1], SLICES), send(packed[0], CHIP), send(packed[1], SLICES ^ CHIP)]
    (mix,) = call(
        lambda *r: gates_kernel(window, capacity, *r), "gates",
        [jax.ShapeDtypeStruct((3, window, capacity, token_count), BF16)],
        (plane, ids_t, levels_t), [SMEM, VMEM, VMEM],
    )

    def ffn(pieces, name):
        mine = jnp.concatenate(pieces, 0) if len(pieces) > 1 else pieces[0]
        other = send(mine, CORE)
        n = mine.shape[0]
        keep, give = call(
            lambda *r: ffn_kernel(2, *r), name, [shape(n, F32), shape(n)],
            (mine, other, gate_w, up_w, down_w), None,
            12 * n * width * hidden_width, 9 << 20,
        )
        return keep + send(give, CORE).astype(F32)

    total = ffn(near, "ffn_near")
    c = capacity
    parts = [total[i * c : (i + 1) * c].astype(BF16) for i in range(4)]
    owners = [0, 0, 1, 1]
    pieces = [parts[0], send(parts[2], CHIP), send(parts[1], SLICES), send(parts[3], SLICES ^ CHIP)]
    for g in groups:
        own = jnp.concatenate([landed[k] for k in g], 0) if len(g) > 1 else landed[g[0]]
        across = send(own, CHIP)
        total = ffn([own, across], "ffn_far")
        n = own.shape[0]
        merged = (total[:n] + send(total[n:].astype(BF16), CHIP).astype(F32)).astype(BF16)
        for i, k in enumerate(g):
            owners.append(k)
            pieces.append(send(merged[i * c : (i + 1) * c], k * SLICES))
    return call(
        lambda *r: combine_kernel(owners, *r), "combine", shape(token_count), (mix, *pieces), None,
        6 * len(owners) * capacity * token_count * width,
    )


def solution(mesh):
    rows = P(("groups", "expert"), None)
    blocks = P("expert", None, None)
    return jax.shard_map(
        shards, mesh=mesh, in_specs=(rows, rows, rows, blocks, blocks, blocks), out_specs=rows, check_vma=False
    )
```
